32 devices in a mesh: dp: 8 (over y, x, core), tensor: 4 (over z).
Axes of the slice: x: 2, y: 2, z: 4, core: 2. Of those that a mesh axis runs over, the one named last changes fastest.
Arguments:
- inputs: bfloat16 [16384, 768], P(('dp', 'tensor')), may hold values from -6 to 6
- pass_ids: int32 [16384], P(('dp', 'tensor')), may hold values from 0 to 4
- token_pos: int32 [8, 2048], P('dp'), may hold values from 0 to 1023, never falling along the last dimension, each value on 1 to 5 neighbouring positions
- pass_table: float32 [5, 768], replicated, may hold values from -3 to 3
- ln1_gain: float32 [768], replicated, may hold values from 0.5 to 1.5
- ln1_bias: float32 [768], replicated, may hold values from -2 to 2
- w_qkv: bfloat16 [768, 3, 768], P(None, None, 'tensor'), may hold values from -0.21875 to 0.21875
- q_bias: float32 [768], P('tensor'), may hold values from -3 to 3
- v_bias: float32 [768], P('tensor'), may hold values from -0.2 to 0.2
- w_out: bfloat16 [768, 768], P('tensor'), may hold values from -3 to 3
- out_bias: float32 [768], replicated, may hold values from -2 to 2
- ln2_gain: float32 [768], replicated, may hold values from 0.5 to 1.5
- ln2_bias: float32 [768], replicated, may hold values from -2 to 2
- w_up: bfloat16 [768, 3072], P(None, 'tensor'), may hold values from -0.21875 to 0.21875
- up_bias: float32 [3072], P('tensor'), may hold values from -3 to 3
- w_down: bfloat16 [3072, 768], P('tensor'), may hold values from -0.109375 to 0.109375
- down_bias: float32 [768], replicated, may hold values from -2 to 2
- cotangent: bfloat16 [16384, 768], P(('dp', 'tensor')), may hold values from -6 to 6
Outputs:
- output: bfloat16 [16384, 768], P(('dp', 'tensor'))
- input_grad: float32 [16384, 768], P(('dp', 'tensor'))
- pass_table_grad: float32 [5, 768], replicated
- ln1_gain_grad: float32 [768], replicated
- ln1_bias_grad: float32 [768], replicated
- w_qkv_grad: float32 [768, 3, 768], P(None, None, 'tensor')
- q_bias_grad: float32 [768], P('tensor')
- v_bias_grad: float32 [768], P('tensor')
- w_out_grad: float32 [768, 768], P('tensor')
- out_bias_grad: float32 [768], replicated
- ln2_gain_grad: float32 [768], replicated
- ln2_bias_grad: float32 [768], replicated
- w_up_grad: float32 [768, 3072], P(None, 'tensor')
- up_bias_grad: float32 [3072], P('tensor')
- w_down_grad: float32 [3072, 768], P('tensor')
- down_bias_grad: float32 [768], replicated
The draws below stay inside these ranges and needn't reach their ends.
Inputs may be any that keep to these rules, and one draw needn't show every extreme that they name: Along each sequence token_pos never falls, and each value stands at 1 to 5 consecutive rows.
All inputs are finite; a program needn't handle non-finite values.
Results may differ from the reference program's by a relative error of at most 0.012.
Values may be sent and summed in bfloat16 or wider, within the bound.
A program may use at most 128 MiB of HBM per device.

```python
import math
import jax
import jax.numpy as jnp
import numpy as np
from jax import lax

D = 768
HEADS = 12
FF = 3072
PASSES = 5
LEN = 2048
SEQS = 8
ROWS = 16384


def touch_ends(entries, stream_key, smallest, top_value):
    longest = entries.shape.index(max(entries.shape))
    spots = []
    for shift in (0, 1):
        where = [jax.random.randint(jax.random.fold_in(stream_key, axis), (), 0, length) for axis, length in enumerate(entries.shape)]
        where[longest] = (where[longest] + shift) % entries.shape[longest]
        spots.append(tuple(where))
    return entries.at[spots[0]].set(smallest).at[spots[1]].set(top_value)


def block_levels(own_key, dims, split, smallest, high):
    level = 1.0
    for axis_at, shards_of in split:
        heights = jax.random.uniform(jax.random.fold_in(jax.random.fold_in(own_key, 6), axis_at), (shards_of,), jnp.float32, smallest / len(split), high / len(split))
        level = level * jnp.repeat(jnp.exp(heights), dims[axis_at] // shards_of).reshape((-1,) + (1,) * (len(dims) - 1 - axis_at))
    return level


def length_profile(count, total, reach, slope):
    portions = [(1 << 20) // math.isqrt(grade ** slope) + 1 for grade in range(2, count + 1)]
    surplus, given = total - reach - (count - 1), [1] * (count - 1)
    while surplus > 0:
        movable = [i for i in range(count - 1) if given[i] < reach]
        pool, left = sum([portions[i] for i in movable]), surplus
        for i in movable:
            more = min(reach - given[i], max(1, left * portions[i] // pool), surplus)
            given[i] = given[i] + more
            surplus = surplus - more
    return np.array([reach] + given)


def uneven(own_key, amount, total, limit, lean):
    if amount == 2:
        one = jax.random.randint(own_key, (), max(1, total - limit), min(limit, total - 1) + 1)
        return jnp.stack([one, total - one])
    tallies = jnp.asarray(length_profile(amount, total, limit, lean), jnp.int32)
    pairs = (amount - 1) // 2
    donor, sink = tallies[1:1 + 2 * pairs:2], tallies[2:2 + 2 * pairs:2]
    slack = jnp.minimum(donor - 1, limit - sink)
    moved = jax.random.randint(jax.random.fold_in(own_key, 1), (pairs,), 0, 1 << 20) % (slack + 1)
    tallies = tallies.at[1:1 + 2 * pairs:2].set(donor - moved).at[2:2 + 2 * pairs:2].set(sink + moved)
    return tallies[jax.random.permutation(jax.random.fold_in(own_key, 2), amount)]


def centred(key, extent, scale, reach, cuts=(), kind=jnp.bfloat16):
    loudness = block_levels(key, extent, cuts, -0.22, 0.18) if cuts else 1.0
    values = jax.random.normal(key, extent, jnp.float32) * scale * loudness
    return jnp.minimum(jnp.maximum(values, -reach), reach).astype(kind)


def setup_inputs(seed: int = 0) -> dict:
    arg_keys = jax.random.split(jax.random.key(seed), 19)
    return {
        "inputs": centred(arg_keys[0], (ROWS, D), 1.0, 6.0, ((0, 32),)),
        "pass_ids": touch_ends(jax.random.randint(arg_keys[1], (ROWS,), 0, PASSES), jax.random.fold_in(arg_keys[1], 1), 0, PASSES - 1).astype(jnp.int32),
        "token_pos": jax.vmap(lambda own: jnp.searchsorted(jnp.cumsum(uneven(own, LEN // 2, LEN, 5, 0)), jnp.arange(LEN), side="right"))(jax.random.split(arg_keys[2], SEQS)).reshape((SEQS, LEN)).astype(jnp.int32),
        "pass_table": centred(arg_keys[3], (PASSES, D), 0.5, 3.0, (), jnp.float32),
        "ln1_gain": jnp.clip(1.0 + 0.1 * jax.random.normal(arg_keys[4], (D,), jnp.float32), 0.5, 1.5),
        "ln1_bias": centred(arg_keys[5], (D,), 0.3, 2.0, (), jnp.float32),
        "w_qkv": centred(arg_keys[6], (D, 3, D), D ** -0.5, 0.21875, ((2, 4),)),
        "q_bias": centred(arg_keys[7], (D,), 0.5, 3.0, ((0, 4),), jnp.float32),
        "v_bias": centred(arg_keys[8], (D,), 0.03, 0.2, ((0, 4),), jnp.float32),
        "w_out": centred(arg_keys[9], (D, D), (max(1, D // 192)) ** -0.5, 3.0, ((0, 4),)),
        "out_bias": centred(arg_keys[10], (D,), 0.3, 2.0, (), jnp.float32),
        "ln2_gain": jnp.clip(1.0 + 0.1 * jax.random.normal(arg_keys[11], (D,), jnp.float32), 0.5, 1.5),
        "ln2_bias": centred(arg_keys[12], (D,), 0.3, 2.0, (), jnp.float32),
        "w_up": centred(arg_keys[13], (D, FF), D ** -0.5, 0.21875, ((1, 4),)),
        "up_bias": centred(arg_keys[14], (FF,), 0.5, 3.0, ((0, 4),), jnp.float32),
        "w_down": centred(arg_keys[15], (FF, D), FF ** -0.5, 0.109375, ((0, 4),)),
        "down_bias": centred(arg_keys[16], (D,), 0.3, 2.0, (), jnp.float32),
        "cotangent": centred(arg_keys[17], (ROWS, D), 1.0, 6.0, ((0, 32),)),
    }


highest = lax.Precision.HIGHEST
epsilon = 1e-05

@jax.custom_vjp
def low(v):
    return lax.optimization_barrier(v.astype(jnp.bfloat16)).astype(jnp.float32)

@jax.custom_vjp
def low_back(v):
    return v

def low_keep(v):
    return (low(v), None)

def low_pass(kept, grad):
    return (grad,)

def back_keep(v):
    return (v, None)

def back_low(kept, grad):
    return (low(grad),)
low.defvjp(low_keep, low_pass)
low_back.defvjp(back_keep, back_low)

def matmul(left_mat, right_mat):
    return jnp.dot(left_mat, right_mat, precision=highest, preferred_element_type=jnp.float32)

def layer_norm(values, gains, offsets):
    centered = values - lax.optimization_barrier(jnp.mean(values, axis=-1, keepdims=True))
    variance = lax.optimization_barrier(jnp.mean(centered * centered, axis=-1, keepdims=True))
    return centered * lax.rsqrt(variance + epsilon) * gains + offsets

def attend_block(query_rows, key_rows, value_rows, query_pos, key_pos):
    scores = jnp.einsum('qhd,khd->hqk', query_rows, key_rows, precision=highest)
    scores = low_back(scores)
    visible = key_pos[None, :] <= query_pos[:, None]
    scores = jnp.where(visible[None], scores, -1e+30)
    attn_probs = low(jax.nn.softmax(scores, axis=-1))
    return jnp.einsum('hqk,khd->qhd', attn_probs, value_rows, precision=highest)

def layer_forward(params, inputs_seq, onehot, positions):
    pass_table, ln1_gain, ln1_bias, w_qkv, q_bias, v_bias, w_out, out_bias, ln2_gain, ln2_bias, w_up, up_bias, w_down, down_bias = params
    length = inputs_seq.shape[0]
    head_size = D // HEADS
    hidden = inputs_seq + matmul(onehot, pass_table)
    normed = low(layer_norm(hidden, ln1_gain, ln1_bias))
    queries = low_back(low((matmul(normed, w_qkv[:, 0, :]) + q_bias) * 0.125))
    key_all = low_back(low(matmul(normed, w_qkv[:, 1, :])))
    value_all = low_back(low(matmul(normed, w_qkv[:, 2, :]) + v_bias))
    block_rows = min(512, length)
    block_count = length // block_rows
    query_blocks = queries.reshape(block_count, block_rows, HEADS, head_size)
    key_split = key_all.reshape(length, HEADS, head_size)
    value_split = value_all.reshape(length, HEADS, head_size)

    def one_block(paired):
        return attend_block(paired[0], key_split, value_split, paired[1], positions)
    context = lax.map(jax.checkpoint(one_block), (query_blocks, positions.reshape(block_count, block_rows)))
    context = low_back(low(context.reshape(length, D)))
    attn_out = low_back(matmul(context, w_out) + out_bias)
    resid = hidden + attn_out
    normed2 = low(layer_norm(resid, ln2_gain, ln2_bias))
    pre_act = low_back(matmul(normed2, w_up) + up_bias)
    activ = low(jax.nn.gelu(pre_act, approximate=True))
    mlp_out = low_back(matmul(activ, w_down) + down_bias)
    return resid + mlp_out

def add_trees(first_tree, second_tree):
    return jax.tree.map(jnp.add, first_tree, second_tree)

def reference(inputs, pass_ids, token_pos, pass_table, ln1_gain, ln1_bias, w_qkv, q_bias, v_bias, w_out, out_bias, ln2_gain, ln2_bias, w_up, up_bias, w_down, down_bias, cotangent):
    f32 = jnp.float32
    params = (pass_table, ln1_gain, ln1_bias, w_qkv.astype(f32), q_bias, v_bias, w_out.astype(f32), out_bias, ln2_gain, ln2_bias, w_up.astype(f32), up_bias, w_down.astype(f32), down_bias)
    seq_count, length = token_pos.shape
    inputs_seq = inputs.astype(f32).reshape(seq_count, length, D)
    passes_seq = pass_ids.reshape(seq_count, length)
    grads_seq = cotangent.astype(f32).reshape(seq_count, length, D)

    def step(totals, sequence):
        seq_rows, seq_passes, positions, seq_grads = sequence
        onehot = (seq_passes[:, None] == jnp.arange(PASSES, dtype=jnp.int32)[None, :]).astype(f32)

        def apply(weights, acts):
            return layer_forward(weights, acts, onehot, positions)
        result, pullback = jax.vjp(apply, params, seq_rows)
        weight_grads, row_grads = pullback(seq_grads)
        return (add_trees(totals, weight_grads), (result.astype(jnp.bfloat16), row_grads))
    initial = jax.tree.map(jnp.zeros_like, params)
    totals, (outputs, input_grads) = lax.scan(step, initial, (inputs_seq, passes_seq, token_pos, grads_seq))
    table_grad, ln1_gain_grad, ln1_bias_grad, w_qkv_grad, q_bias_grad, v_bias_grad, w_out_grad, out_bias_grad, ln2_gain_grad, ln2_bias_grad, w_up_grad, up_bias_grad, w_down_grad, down_bias_grad = totals
    return (outputs.reshape(seq_count * length, D), input_grads.reshape(seq_count * length, D), table_grad, ln1_gain_grad, ln1_bias_grad, w_qkv_grad, q_bias_grad, v_bias_grad, w_out_grad, out_bias_grad, ln2_gain_grad, ln2_bias_grad, w_up_grad, up_bias_grad, w_down_grad, down_bias_grad)
```

```python
import functools

import jax
import jax.numpy as jnp
from jax import lax
from jax.experimental import pallas as pl
from jax.experimental.pallas import tpu as pltpu
from jax.sharding import PartitionSpec as P

D = 768
HEADS = 12
HD = D // HEADS
PASSES = 5
EPS = 1e-05
NEG = -1e30
TIES = 128

f32 = jnp.float32
bf16 = jnp.bfloat16
MESH = pl.DeviceIdType.MESH


def dot_nn(a, b):
    return lax.dot_general(a, b, (((1,), (0,)), ((), ())), preferred_element_type=f32)


def dot_nt(a, b):
    return lax.dot_general(a, b, (((1,), (1,)), ((), ())), preferred_element_type=f32)


def dot_tn(a, b):
    return lax.dot_general(a, b, (((0,), (0,)), ((), ())), preferred_element_type=f32)


def head_lanes(h, rows, width):
    lane = lax.broadcasted_iota(jnp.int32, (rows, width), 1)
    return (lane >= h * HD) & (lane < (h + 1) * HD)


def only_head(h, rows):
    return jnp.where(head_lanes(h, *rows.shape), rows, jnp.zeros((), rows.dtype))


def attn_fwd_kernel(
    BQ, x_ref, wq_ref, wk_ref, wv_ref, qb_ref, vb_ref, posr_ref, posc_ref,
    ctx_ref, lse_ref, q_ref, k_ref, v_ref,
):
    length, width = ctx_ref.shape
    heads = width // HD

    def project(i, carry):
        r = pl.ds(pl.multiple_of(i * BQ, BQ), BQ)
        x = x_ref[r, :]
        q_ref[r, :] = ((dot_nn(x, wq_ref[...]) + qb_ref[...]) * 0.125).astype(bf16)
        k_ref[r, :] = dot_nn(x, wk_ref[...]).astype(bf16)
        v_ref[r, :] = (dot_nn(x, wv_ref[...]) + vb_ref[...]).astype(bf16)
        return carry

    lax.fori_loop(0, length // BQ, project, 0)

    def one_head(h, carry):
        for i in range(length // BQ):
            r0, r1 = i * BQ, (i + 1) * BQ
            hi = min(length, r1 + TIES)
            mine = head_lanes(h, BQ, width)
            q = jnp.where(mine, q_ref[r0:r1, :], jnp.zeros((), bf16))
            s1 = dot_nt(q, k_ref[r0:hi, :])
            s1 = jnp.where(posr_ref[:, r0:hi] <= posc_ref[r0:r1, :], s1, NEG)
            m = jnp.max(s1, axis=1, keepdims=True)
            if i:
                s0 = dot_nt(q, k_ref[0:r0, :])
                m = jnp.maximum(m, jnp.max(s0, axis=1, keepdims=True))
            p1 = jnp.exp(s1 - m)
            total = jnp.sum(p1, axis=1, keepdims=True)
            acc = dot_nn(p1.astype(bf16), v_ref[r0:hi, :])
            if i:
                p0 = jnp.exp(s0 - m)
                total = total + jnp.sum(p0, axis=1, keepdims=True)
                acc = acc + dot_nn(p0.astype(bf16), v_ref[0:r0, :])
            out = (acc / total).astype(bf16)
            ctx_ref[r0:r1, :] = jnp.where(mine, out, ctx_ref[r0:r1, :])
            lse_ref[pl.ds(h, 1), r0:r1] = jnp.reshape(m + jnp.log(total), (1, BQ))
        return carry

    ctx_ref[...] = jnp.zeros_like(ctx_ref)
    lax.fori_loop(0, heads, one_head, 0)


def attn_bwd_kernel(
    BQ, q_ref, k_ref, v_ref, g_ref, ctx_ref, posr_ref, posc_ref, lse_ref,
    dq_ref, dk_ref, dv_ref, dka, dva,
):
    length, width = q_ref.shape
    heads = width // HD
    dka[...] = jnp.zeros_like(dka)
    dva[...] = jnp.zeros_like(dva)
    pick = (
        lax.broadcasted_iota(jnp.int32, (8, width), 1) // HD
        == lax.broadcasted_iota(jnp.int32, (8, width), 0)
    ).astype(f32)
    for i in range(length // BQ):
        r0, r1 = i * BQ, (i + 1) * BQ
        hi = min(length, r1 + TIES)
        posr = posr_ref[:, r0:r1]
        g_all, q_all = g_ref[r0:r1, :], q_ref[r0:r1, :]
        prod = g_all.astype(f32) * ctx_ref[r0:r1, :].astype(f32)
        delta = lax.dot_general(
            pick, prod, (((1,), (1,)), ((), ())),
            precision=lax.Precision.HIGHEST, preferred_element_type=f32,
        )
        qs = [only_head(h, q_all) for h in range(heads)]
        gs = [only_head(h, g_all) for h in range(heads)]
        qc, gc = jnp.concatenate(qs, axis=0), jnp.concatenate(gs, axis=0)
        dq = [None] * heads
        for a, b, masked in ([(0, r0, False)] if i else []) + [(r0, hi, True)]:
            ps, dss = [], []
            for h in range(heads):
                st = dot_nt(k_ref[a:b, :], qs[h])
                p = jnp.exp(st - lse_ref[h : h + 1, r0:r1])
                if masked:
                    p = jnp.where(posc_ref[a:b, :] <= posr, p, 0.0)
                dp = dot_nt(v_ref[a:b, :], gs[h])
                ds = (p * (dp - delta[h : h + 1, :])).astype(bf16)
                ps.append(p.astype(bf16))
                dss.append(ds)
                t = dot_tn(ds, k_ref[a:b, :])
                dq[h] = t if dq[h] is None else dq[h] + t
            dva[a:b, :] += dot_nn(jnp.concatenate(ps, axis=1), gc)
            dka[a:b, :] += dot_nn(jnp.concatenate(dss, axis=1), qc)
        out = dq[0]
        for h in range(1, heads):
            out = jnp.where(head_lanes(h, BQ, width), dq[h], out)
        dq_ref[r0:r1, :] = out.astype(bf16) * jnp.asarray(0.125, bf16)
    dk_ref[...] = dka[...].astype(bf16)
    dv_ref[...] = dva[...].astype(bf16)


def in_vmem(n):
    return [pl.BlockSpec(memory_space=pltpu.VMEM)] * n


def attention_forward(x, wq, wk, wv, qb, vb, posr, posc, block):
    length, width = x.shape[0], wq.shape[1]
    s = jax.ShapeDtypeStruct
    area = length * length * width
    return pl.pallas_call(
        functools.partial(attn_fwd_kernel, block),
        out_shape=(
            s((length, width), bf16), s((width // HD, length), f32),
            s((length, width), bf16), s((length, width), bf16), s((length, width), bf16),
        ),
        in_specs=in_vmem(8),
        out_specs=tuple(in_vmem(5)),
        compiler_params=pltpu.CompilerParams(vmem_limit_bytes=56 << 20),
        cost_estimate=pl.CostEstimate(
            flops=12 * area, bytes_accessed=8 << 20, transcendentals=length * length * 2
        ),
        name="attn_fwd",
    )(x, wq, wk, wv, qb, vb, posr, posc)


def attention_backward(q, k, v, g, ctx, posr, posc, lse, block):
    length, width = q.shape
    s = jax.ShapeDtypeStruct
    area = length * length * width
    return pl.pallas_call(
        functools.partial(attn_bwd_kernel, block),
        out_shape=(s((length, width), bf16),) * 3,
        in_specs=in_vmem(8),
        out_specs=tuple(in_vmem(3)),
        scratch_shapes=[pltpu.VMEM((length, width), f32), pltpu.VMEM((length, width), f32)],
        compiler_params=pltpu.CompilerParams(vmem_limit_bytes=56 << 20),
        cost_estimate=pl.CostEstimate(
            flops=20 * area, bytes_accessed=8 << 20, transcendentals=length * length * 2
        ),
        name="attn_bwd",
    )(q, k, v, g, ctx, posr, posc, lse)


def swap_kernel(n, x_ref, o_ref, own_sem, send_sem, recv_sem):
    me = lax.axis_index("tensor")
    dp = lax.axis_index("dp")
    peers = [lax.rem(me + k, n) for k in range(1, n)]
    barrier = pltpu.get_barrier_semaphore()
    for peer in peers:
        pl.semaphore_signal(barrier, inc=1, device_id=(dp, peer), device_id_type=MESH)
    pl.semaphore_wait(barrier, n - 1)
    own = pltpu.make_async_copy(x_ref.at[me], o_ref.at[me], own_sem)
    copies = [
        pltpu.make_async_remote_copy(
            src_ref=x_ref.at[peer], dst_ref=o_ref.at[me],
            send_sem=send_sem.at[k], recv_sem=recv_sem.at[k],
            device_id=(dp, peer), device_id_type=MESH,
        )
        for k, peer in enumerate(peers)
    ]
    for copy in copies:
        copy.start()
    own.start()
    own.wait()
    for copy in copies:
        copy.wait()


def swap(x, collective_id):
    n = x.shape[0]
    return pl.pallas_call(
        functools.partial(swap_kernel, n),
        out_shape=jax.ShapeDtypeStruct(x.shape, x.dtype),
        in_specs=[pl.BlockSpec(memory_space=pl.ANY)],
        out_specs=pl.BlockSpec(memory_space=pl.ANY),
        scratch_shapes=[
            pltpu.SemaphoreType.DMA, pltpu.SemaphoreType.DMA((n - 1,)),
            pltpu.SemaphoreType.DMA((n - 1,)),
        ],
        compiler_params=pltpu.CompilerParams(collective_id=collective_id, has_side_effects=True),
        cost_estimate=pl.CostEstimate(flops=0, bytes_accessed=32 << 20, transcendentals=0),
        name=f"swap{collective_id}",
    )(x)


def norm_stats(values):
    centered = values - jnp.mean(values, axis=-1, keepdims=True)
    inv = lax.rsqrt(jnp.mean(centered * centered, axis=-1, keepdims=True) + EPS)
    return centered * inv, inv


def norm_back(grad, n, inv, gain):
    e = grad * gain
    dv = inv * (
        e - jnp.mean(e, axis=-1, keepdims=True) - n * jnp.mean(e * n, axis=-1, keepdims=True)
    )
    return dv, jnp.sum(grad * n, axis=0), jnp.sum(grad, axis=0)


def gelu_parts(u):
    c = 0.7978845608028654
    t = jnp.tanh(c * (u + 0.044715 * u * u * u))
    act = 0.5 * u * (1.0 + t)
    slope = 0.5 * (1.0 + t) + 0.5 * u * (1.0 - t * t) * c * (1.0 + 3 * 0.044715 * u * u)
    return act, slope


def on_device(
    inputs, pass_ids, token_pos, pass_table, ln1_gain, ln1_bias, w_qkv, q_bias, v_bias, w_out,
    out_bias, ln2_gain, ln2_bias, w_up, up_bias, w_down, down_bias, cotangent, *, nt, nd,
):
    width = w_qkv.shape[2]
    length = token_pos.shape[1]
    rows = inputs.shape[0]
    hid = w_up.shape[1]
    everyone = ("tensor", "dp")
    dpi = lax.axis_index("dp")

    onehot = (pass_ids[:, None] == jnp.arange(PASSES, dtype=jnp.int32)[None, :]).astype(f32)
    hidden = inputs.astype(f32)
    for p in range(PASSES):
        hidden = hidden + jnp.where((pass_ids == p)[:, None], pass_table[p][None, :], 0.0)
    n1, inv1 = norm_stats(hidden)
    normed = (n1 * ln1_gain + ln1_bias).astype(bf16)
    normed_all = lax.all_gather(normed, "tensor", axis=0, tiled=True)

    def whole(w):
        part = w.shape[0] // nd
        mine = lax.dynamic_slice_in_dim(w, dpi * part, part, 0)
        return lax.all_gather(mine, everyone, axis=0, tiled=True)

    w_out_all = whole(w_out)
    w_up_all = whole(w_up).reshape(nt, D, hid)
    w_down_all = whole(w_down)
    up_bias_all = lax.all_gather(up_bias, "tensor", axis=0, tiled=True)

    posr, posc = token_pos.reshape(1, length), token_pos.reshape(length, 1)
    wq, wk, wv = w_qkv[:, 0, :], w_qkv[:, 1, :], w_qkv[:, 2, :]
    ctx, lse, q, k, v = attention_forward(
        normed_all, wq, wk, wv, q_bias[None, :], v_bias[None, :], posr, posc, 256
    )
    mine = swap(ctx.reshape(nt, rows, width), 1)
    context = jnp.transpose(mine, (1, 0, 2)).reshape(rows, D)

    resid = hidden + dot_nn(context, w_out_all) + out_bias
    n2, inv2 = norm_stats(resid)
    normed2 = (n2 * ln2_gain + ln2_bias).astype(bf16)
    acts, slopes = [], []
    for z in range(nt):
        u = dot_nn(normed2, w_up_all[z]) + up_bias_all[z * hid : (z + 1) * hid]
        a, s = gelu_parts(u)
        acts.append(a.astype(bf16))
        slopes.append(s)
    activ = jnp.concatenate(acts, axis=1)
    slope = jnp.concatenate(slopes, axis=1)
    output = (resid + dot_nn(activ, w_down_all) + down_bias).astype(bf16)
    grad_out = cotangent.astype(f32)
    down_bias_part = jnp.sum(grad_out, axis=0)
    w_down_part = dot_tn(activ, cotangent)
    grad_pre = (dot_nt(cotangent, w_down_all) * slope).astype(bf16)
    up_bias_part = jnp.sum(grad_pre.astype(f32), axis=0)
    w_up_parts = [dot_tn(normed2, grad_pre[:, z * hid : (z + 1) * hid]) for z in range(nt)]
    w_up_part = jnp.concatenate(w_up_parts, axis=0)
    grad_norm2 = jnp.zeros((rows, D), f32)
    for z in range(nt):
        grad_norm2 = grad_norm2 + dot_nt(grad_pre[:, z * hid : (z + 1) * hid], w_up_all[z])
    back2, ln2_gain_part, ln2_bias_part = norm_back(grad_norm2, n2, inv2, ln2_gain)
    grad_resid = grad_out + back2
    grad_attn = grad_resid.astype(bf16)
    out_bias_part = jnp.sum(grad_attn.astype(f32), axis=0)
    w_out_part = dot_tn(context, grad_attn)
    grad_context = dot_nt(grad_attn, w_out_all).astype(bf16)
    send = jnp.transpose(grad_context.reshape(rows, nt, width), (1, 0, 2))
    g = swap(send, 2).reshape(length, width)

    def reduced(part):
        shard = lax.psum_scatter(
            part.astype(bf16), everyone, scatter_dimension=0, tiled=True
        )
        return lax.all_gather(shard, "dp", axis=0, tiled=True).astype(f32)

    w_down_grad = reduced(w_down_part)
    w_up_grad = reduced(w_up_part)
    w_out_grad = reduced(w_out_part)

    dq, dk, dv = attention_backward(q, k, v, g, ctx, posr, posc, lse, 256)
    share = dot_nt(dq, wq) + dot_nt(dk, wk) + dot_nt(dv, wv)
    grad_norm1 = lax.psum_scatter(
        share.astype(bf16), "tensor", scatter_dimension=0, tiled=True
    ).astype(f32)
    w_qkv_grad = jnp.stack([dot_tn(normed_all, t) for t in (dq, dk, dv)], axis=1)
    q_bias_grad = jnp.sum(dq.astype(f32), axis=0)
    v_bias_grad = jnp.sum(dv.astype(f32), axis=0)
    back1, ln1_gain_part, ln1_bias_part = norm_back(grad_norm1, n1, inv1, ln1_gain)
    input_grad = grad_resid + back1
    table_part = lax.dot_general(
        onehot, input_grad, (((0,), (0,)), ((), ())),
        precision=lax.Precision.HIGHEST, preferred_element_type=f32,
    )
    w_qkv_grad, q_bias_grad, v_bias_grad = lax.psum((w_qkv_grad, q_bias_grad, v_bias_grad), "dp")
    (
        table_grad, ln1_gain_grad, ln1_bias_grad, out_bias_grad, ln2_gain_grad, ln2_bias_grad,
        down_bias_grad, up_bias_all_grad,
    ) = lax.psum(
        (
            table_part, ln1_gain_part, ln1_bias_part, out_bias_part, ln2_gain_part, ln2_bias_part,
            down_bias_part, up_bias_part,
        ),
        ("dp", "tensor"),
    )
    up_bias_grad = lax.dynamic_slice_in_dim(
        up_bias_all_grad, lax.axis_index("tensor") * hid, hid, 0
    )
    return (
        output, input_grad, table_grad, ln1_gain_grad, ln1_bias_grad, w_qkv_grad, q_bias_grad,
        v_bias_grad, w_out_grad, out_bias_grad, ln2_gain_grad, ln2_bias_grad, w_up_grad,
        up_bias_grad, w_down_grad, down_bias_grad,
    )


def solution(mesh):
    both = ("dp", "tensor")
    in_specs = (
        P(both, None), P(both), P("dp", None), P(), P(), P(), P(None, None, "tensor"),
        P("tensor"), P("tensor"), P("tensor", None), P(), P(), P(), P(None, "tensor"),
        P("tensor"), P("tensor", None), P(), P(both, None),
    )
    out_specs = (
        P(both, None), P(both, None), P(), P(), P(), P(None, None, "tensor"), P("tensor"),
        P("tensor"), P("tensor", None), P(), P(), P(), P(None, "tensor"), P("tensor"),
        P("tensor", None), P(),
    )
    body = functools.partial(on_device, nt=mesh.shape["tensor"], nd=mesh.shape["dp"])
    return jax.shard_map(
        body, mesh=mesh, in_specs=in_specs, out_specs=out_specs, check_vma=False
    )
```
